32 devices in a mesh: gz: 4 (over z), gy: 2 (over x), vec: 4 (over y, core).
Axes of the slice: x: 2, y: 2, z: 4, core: 2. Of those that a mesh axis runs over, the one named last changes fastest.
Arguments:
- vectors: bfloat16 [256, 3, 32, 4, 128], P('vec', None, 'gz', 'gy'), may hold values from -6 to 6
- links: bfloat16 [3, 3, 3, 32, 4, 128], P(None, None, None, 'gz', 'gy'), may hold values from -4 to 4
- momentum: int32 [3], replicated, may hold values from -5 to 5, as said below
- directions: int32 [3], replicated, may hold values from 0 to 2, each once
Outputs:
- elementals: float32 [4, 2, 256, 256], P(None, None, 'vec')
The draws below stay inside these ranges and needn't reach their ends.
Inputs may be any that keep to these rules, and one draw needn't show every extreme that they name: `momentum`: one component is -5, another 5. `directions`: each of 0, 1, 2 once.
All inputs are finite; a program needn't handle non-finite values.
Results may differ from the reference program's by a relative error of at most 0.0029.
Values may be sent and summed in bfloat16 or wider, within the bound.
A program may use at most 128 MiB of HBM per device.

```python
import math
import jax
import jax.numpy as jnp
from jax import lax

NEV = 256
LX = 64
NY = 4
NZ = 32


def draw_momentum(key, part):
    first_key = jax.random.fold_in(key, 11)
    second_key = jax.random.fold_in(key, 23)
    middle = jax.random.randint(first_key, (1,), -5, 6, dtype=jnp.int32)
    values = jnp.concatenate([jnp.array([-5, 5], dtype=jnp.int32), middle])
    order = jax.random.permutation(second_key, 3)
    return values[order].astype(jnp.int32)


def block_scale(stream_key, extent, cuts, smallest, largest):
    loudness, own = 1.0, jax.random.fold_in(stream_key, 6)
    for position, blocks in cuts:
        heights = jnp.exp(jax.random.uniform(jax.random.fold_in(own, position), (blocks,), jnp.float32, smallest / len(cuts), largest / len(cuts)))
        loudness = loudness * jnp.repeat(heights, extent[position] // blocks).reshape([-1 if axis == position else 1 for axis in range(len(extent))])
    return loudness


def gaussian(stream_key, dims, deviation, bound, pieces=(), kind=jnp.bfloat16):
    factor_of = block_scale(stream_key, dims, pieces, -0.22, 0.18) if pieces else 1.0
    drawn = jax.random.normal(stream_key, dims, jnp.float32) * deviation * factor_of
    return jnp.minimum(jnp.maximum(drawn, -bound), bound).astype(kind)


def setup_inputs(seed: int = 0) -> dict:
    arg_keys = jax.random.split(jax.random.key(seed), 5)
    return {
        "vectors": gaussian(arg_keys[0], (NEV, 3, NZ, NY, 2 * LX), 1.0, 6.0, ((0, 4), (2, 4), (3, 2))),
        "links": gaussian(arg_keys[1], (3, 3, 3, NZ, NY, 2 * LX), 0.58, 4.0, ((3, 4), (4, 2))),
        "momentum": draw_momentum(jax.random.fold_in(arg_keys[4], 71), 0),
        "directions": jax.random.permutation(arg_keys[3], 3).astype(jnp.int32),
    }


def apply_link(link_pair, field_pair):
    link_real, link_imag = link_pair
    field_real, field_imag = field_pair
    out_real = 0.0
    out_imag = 0.0
    for column in range(3):
        coeff_real = link_real[:, column][None]
        coeff_imag = link_imag[:, column][None]
        value_real = field_real[:, column][:, None]
        value_imag = field_imag[:, column][:, None]
        out_real = out_real + coeff_real * value_real - coeff_imag * value_imag
        out_imag = out_imag + coeff_real * value_imag + coeff_imag * value_real
    return (out_real, out_imag)

def apply_adjoint(link_pair, field_pair):
    link_real, link_imag = link_pair
    field_real, field_imag = field_pair
    out_real = 0.0
    out_imag = 0.0
    for column in range(3):
        coeff_real = link_real[column][None]
        coeff_imag = link_imag[column][None]
        value_real = field_real[:, column][:, None]
        value_imag = field_imag[:, column][:, None]
        out_real = out_real + coeff_real * value_real + coeff_imag * value_imag
        out_imag = out_imag + coeff_real * value_imag - coeff_imag * value_real
    return (out_real, out_imag)

def covariant(up_pair, down_pair, ahead_pair, behind_pair):
    forward = apply_link(up_pair, ahead_pair)
    backward = apply_adjoint(down_pair, behind_pair)
    return (0.5 * (forward[0] - backward[0]), 0.5 * (forward[1] - backward[1]))

def phase_table(momentum, x_coords, y_coords, z_coords, extent_x, extent_y, extent_z):
    frac_x = (momentum[0] * x_coords % extent_x).astype(jnp.float32) / extent_x
    frac_y = (momentum[1] * y_coords % extent_y).astype(jnp.float32) / extent_y
    frac_z = (momentum[2] * z_coords % extent_z).astype(jnp.float32) / extent_z
    summed = frac_z[:, None, None] + frac_y[None, :, None] + frac_x[None, None, :]
    angle = 2.0 * math.pi * summed
    return (jnp.cos(angle), jnp.sin(angle))

def make_operators(field_pair, ahead_list, behind_list, up_list, down_list, directions, cosine, sine):
    derived = [covariant(up_list[axis_number], down_list[axis_number], ahead_list[axis_number], behind_list[axis_number]) for axis_number in range(3)]
    results = []
    for op_slot in range(3):
        chosen = directions[op_slot]
        real_part = jnp.where(chosen == 0, derived[0][0], jnp.where(chosen == 1, derived[1][0], derived[2][0]))
        imag_part = jnp.where(chosen == 0, derived[0][1], jnp.where(chosen == 1, derived[1][1], derived[2][1]))
        results.append(jnp.stack([real_part, imag_part], -2).astype(jnp.bfloat16))
    field_real, field_imag = field_pair
    phased_real = field_real * cosine + field_imag * sine
    phased_imag = field_imag * cosine - field_real * sine
    results.append(jnp.stack([phased_real, phased_imag], -2).astype(jnp.bfloat16))
    return jnp.stack(results, 1)

def contract(rows, stacked_left):
    row_count = rows.shape[0]
    flat_rows = rows.reshape(row_count * 4, -1)
    product = lax.dot_general(flat_rows, stacked_left, (((1,), (1,)), ((), ())), preferred_element_type=jnp.float32)
    return product.reshape(row_count, 4, 2, stacked_left.shape[0] // 2)

def reference(vectors, links, momentum, directions):
    six_dims = vectors.reshape(NEV, 3, NZ, NY, 2, LX)
    swapped = jnp.stack([-six_dims[..., 1, :], six_dims[..., 0, :]], -2)
    stacked_left = jnp.concatenate([vectors.reshape(NEV, -1), swapped.reshape(NEV, -1)], 0)
    link_wide = links.astype(jnp.float32).reshape(3, 3, 3, NZ, NY, 2, LX)
    up_list = [(link_wide[axis_number, ..., 0, :], link_wide[axis_number, ..., 1, :]) for axis_number in range(3)]
    down_list = [(jnp.roll(up_list[axis_number][0], 1, axis=-1 - axis_number), jnp.roll(up_list[axis_number][1], 1, axis=-1 - axis_number)) for axis_number in range(3)]
    cosine, sine = phase_table(momentum, jnp.arange(LX, dtype=jnp.int32), jnp.arange(NY, dtype=jnp.int32), jnp.arange(NZ, dtype=jnp.int32), LX, NY, NZ)
    block_size = NEV // 16

    def one_block(block_index):
        first_row = (block_index * block_size).astype(jnp.int32)
        block = lax.dynamic_slice_in_dim(vectors, first_row, block_size, 0)
        widened = block.astype(jnp.float32).reshape(block_size, 3, NZ, NY, 2, LX)
        field_real = widened[..., 0, :]
        field_imag = widened[..., 1, :]
        ahead_list = [(jnp.roll(field_real, -1, axis=-1 - axis_number), jnp.roll(field_imag, -1, axis=-1 - axis_number)) for axis_number in range(3)]
        behind_list = [(jnp.roll(field_real, 1, axis=-1 - axis_number), jnp.roll(field_imag, 1, axis=-1 - axis_number)) for axis_number in range(3)]
        transformed = make_operators((field_real, field_imag), ahead_list, behind_list, up_list, down_list, directions, cosine, sine)
        return contract(transformed.reshape(block_size, 4, -1), stacked_left)
    blocks = lax.map(one_block, jnp.arange(16, dtype=jnp.int32))
    summed = blocks.reshape(NEV, 4, 2, NEV) * (1.0 / math.sqrt(LX * NY * NZ))
    return jnp.transpose(summed, (1, 2, 0, 3))
```

```python
import functools
import math

import jax
import jax.numpy as jnp
from jax import lax
from jax.experimental import pallas as pl
from jax.experimental.pallas import tpu as pltpu
from jax.sharding import PartitionSpec as P

MESH = pl.DeviceIdType.MESH


def split_chunks(depth, most):
    count = most
    while depth % count or (depth // count) % 2:
        count -= 1
    return count


def kernel(
    sizes,
    momentum_in,
    directions_in,
    v_ref,
    links_ref,
    out_ref,
    left,
    halo_y,
    halo_z,
    rim_y,
    rim_z,
    tab_x,
    tab_y,
    tab_z,
    edge_y,
    edge_z,
    cos_ref,
    sin_ref,
    trans_a,
    trans_b,
    acc,
    momentum_ref,
    directions_ref,
    outgo,
    income,
    reduced,
    gathered,
    cross_out,
    cross_in,
    back_out,
    back_in,
    local_sem,
    send_sem,
    recv_sem,
    red_sem,
    cross_sem,
):
    gz_n, gy_n, vec_n, depth, height, rows, width, chunks = sizes
    lanes = 2 * width
    two = 2 * rows
    me_z = lax.axis_index("gz")
    me_y = lax.axis_index("gy")
    me_v = lax.axis_index("vec")
    pair = me_v // 2
    side = lax.rem(me_v, 2)
    group = gz_n * gy_n
    me_g = me_z * gy_n + me_y
    span = depth // chunks
    share = rows // group
    partners = [me_v, pair * 2 + 1 - side, (1 - pair) * 2 + side, (1 - pair) * 2 + 1 - side]

    def member(step):
        return lax.rem(me_g + step, group)

    def place(g, k=0):
        return {"gz": g // gy_n, "gy": lax.rem(g, gy_n), "vec": partners[k]}

    barrier = pltpu.get_barrier_semaphore()
    for k in range(vec_n):
        for step in range(group):
            if k or step:
                pl.semaphore_signal(
                    barrier, inc=1, device_id=place(member(step), k), device_id_type=MESH
                )
    scalars = [
        pltpu.make_async_copy(momentum_in, momentum_ref, local_sem.at[0]),
        pltpu.make_async_copy(directions_in, directions_ref, local_sem.at[1]),
    ]
    for copy in scalars:
        copy.start()

    lane = lax.broadcasted_iota(jnp.int32, (1, lanes), 1)
    low_half = lane < width
    last_mask = lax.rem(lane, width) == width - 1
    first_mask = lax.rem(lane, width) == 0
    sign = jnp.where(low_half, 1.0, -1.0).astype(jnp.float32)
    tile = 32 if rows % 32 == 0 else rows

    def coefficients(raw):
        value = raw.astype(jnp.float32) * 0.5
        swapped = pltpu.roll(value, width, 1)
        real = jnp.where(low_half, value, swapped)
        imag = jnp.where(low_half, -swapped, value)
        return real, imag

    def put(table, where, pair_of):
        table[where + (slice(0, 9),)] = pair_of[0]
        table[where + (slice(16, 25),)] = pair_of[1]

    def step_back(value):
        one = pltpu.roll(value, 1, 1)
        other = pltpu.roll(value, width + 1, 1)
        return jnp.where(first_mask, other, one)

    @pl.loop(0, depth)
    def _(z):
        for y in range(height):
            real, imag = coefficients(links_ref[0, z, y])
            put(tab_x, (0, z, y), (real, imag))
            put(tab_x, (1, z, y), (step_back(real), step_back(imag)))
            put(tab_y, (z, y), coefficients(links_ref[1, z, y]))
            put(tab_z, (z, y), coefficients(links_ref[2, z, y]))

    for copy in scalars:
        copy.wait()
    site_shape = (depth * height, lanes)
    site = lax.broadcasted_iota(jnp.int32, site_shape, 0)
    x_at = lax.rem(lax.broadcasted_iota(jnp.int32, site_shape, 1), width)
    y_at = me_y * height + lax.rem(site, height)
    z_at = me_z * depth + site // height

    def fraction(component, at, extent):
        turned = lax.rem(momentum_ref[component] * at, extent)
        turned = jnp.where(turned < 0, turned + extent, turned)
        return turned.astype(jnp.float32) / extent

    angle = (2.0 * math.pi) * (
        fraction(2, z_at, depth * gz_n)
        + fraction(1, y_at, height * gy_n)
        + fraction(0, x_at, width)
    )
    cos_ref[...] = jnp.cos(angle)
    sin_ref[...] = jnp.sin(angle) * sign

    pl.semaphore_wait(barrier, group * vec_n - 1)

    counter = [0]

    def remote(src, dst, device):
        index = counter[0]
        counter[0] += 1
        return pltpu.make_async_remote_copy(
            src_ref=src,
            dst_ref=dst,
            send_sem=send_sem.at[index],
            recv_sem=recv_sem.at[index],
            device_id=device,
            device_id_type=MESH,
        )

    z_up = {"gz": lax.rem(me_z + 1, gz_n)}
    z_down = {"gz": lax.rem(me_z + gz_n - 1, gz_n)}
    y_up = {"gy": lax.rem(me_y + 1, gy_n)}
    y_down = {"gy": lax.rem(me_y + gy_n - 1, gy_n)}
    sibling = {"vec": partners[1]}
    rim_y_copy = remote(links_ref.at[1, :, height - 1], rim_y, y_up)
    rim_z_copy = remote(links_ref.at[2, depth - 1], rim_z, z_up)
    z_copies = [
        remote(v_ref.at[depth - 1 if y % 2 else 0, y], halo_z.at[y], z_up if y % 2 else z_down)
        for y in range(height)
    ]
    y_copies = [
        remote(v_ref.at[z, height - 1 if z % 2 else 0], halo_y.at[z], y_up if z % 2 else y_down)
        for z in range(depth)
    ]
    near = remote(v_ref, left.at[0], sibling)
    far, relay = [], []
    for k in range(chunks):
        part = pl.ds(k * span, span)
        far.append(remote(v_ref.at[part], left.at[1, part], {"vec": partners[2]}))
        relay.append(remote(left.at[1, part], left.at[2, part], sibling))
    far[0].start()
    rim_y_copy.start()
    rim_z_copy.start()
    for copy in z_copies:
        copy.start()
    for copy in y_copies + far[1:]:
        copy.start()
    near.start()

    def store(ref, where, slot, lo, value):
        turned = pltpu.roll(value, width, 1) * sign
        ref[where + (pl.ds(slot * two + lo, tile),)] = value.astype(jnp.bfloat16)
        ref[where + (pl.ds(slot * two + rows + lo, tile),)] = turned.astype(jnp.bfloat16)

    def load(z, y, colour, lo):
        return v_ref[z, y, colour, pl.ds(lo, tile)].astype(jnp.float32)

    def stencil(ref, where, lo, slot, ahead, behind, up, down):
        sums = [0.0, 0.0, 0.0]
        for col in range(3):
            value, swapped = ahead(col)
            for row in range(3):
                k = row * 3 + col
                sums[row] = sums[row] + (up(k) * value + up(16 + k) * swapped)
        for col in range(3):
            value, swapped = behind(col)
            for row in range(3):
                k = col * 3 + row
                sums[row] = sums[row] + (down(16 + k) * swapped - down(k) * value)
        for row in range(3):
            store(ref, where + (row,), slot, lo, sums[row])

    def swap(value):
        return value, pltpu.roll(value, width, 1)

    def pass_x(z):
        for y in range(height):
            for lo in range(0, rows, tile):
                here = pl.ds(z * height + y, 1)
                cosine = cos_ref[here]
                sine = sin_ref[here]

                def ahead(col):
                    value = load(z, y, col, lo)
                    one = pltpu.roll(value, lanes - 1, 1)
                    other = pltpu.roll(value, width - 1, 1)
                    return jnp.where(last_mask, other, one), jnp.where(last_mask, one, other)

                def behind(col):
                    value = load(z, y, col, lo)
                    one = pltpu.roll(value, 1, 1)
                    other = pltpu.roll(value, width + 1, 1)
                    return jnp.where(first_mask, other, one), jnp.where(first_mask, one, other)

                stencil(
                    trans_a, (z, y), lo, 0, ahead, behind,
                    lambda k: tab_x[0, z, y, k : k + 1],
                    lambda k: tab_x[1, z, y, k : k + 1],
                )
                for col in range(3):
                    value, swapped = swap(load(z, y, col, lo))
                    store(trans_a, (z, y, col), 1, lo, value * cosine + swapped * sine)

    def halo(ref, at):
        return lambda col, lo: ref[at, col, pl.ds(lo, tile)].astype(jnp.float32)

    def inside(z, y):
        return lambda col, lo: load(z, y, col, lo)

    def derive(z, y, slot, ahead, behind, up, down):
        for lo in range(0, rows, tile):
            stencil(
                trans_b, (z, y // 2), lo, slot,
                lambda col: swap(ahead(col, lo)),
                lambda col: swap(behind(col, lo)),
                up,
                down,
            )

    def table(ref, where):
        return lambda k: ref[where + (slice(k, k + 1),)]

    def derive_z(z, y, ahead=None, behind=None, down=None):
        derive(
            z, y, 0,
            ahead or inside(z + 1, y),
            behind or inside(z - 1, y),
            table(tab_z, (z, y)),
            down or table(tab_z, (z - 1, y)),
        )

    def derive_y(z, y):
        top, bottom = y == height - 1, y == 0
        derive(
            z, y, 1,
            halo(halo_y, z) if top else inside(z, y + 1),
            halo(halo_y, z) if bottom else inside(z, y - 1),
            table(tab_y, (z, y)),
            table(edge_y, (z,)) if bottom else table(tab_y, (z, y - 1)),
        )

    def pass_z(t):
        for y in range(0, height, 2):
            derive_z(2 * t + 1, y)
        for y in range(1, height, 2):
            derive_z(2 * t + 2, y)

    def pass_z_edges():
        for y in range(1, height, 2):
            derive_z(0, y, behind=halo(halo_z, y), down=table(edge_z, (y,)))
        for y in range(0, height, 2):
            derive_z(depth - 1, y, ahead=halo(halo_z, y))

    def pass_y(t):
        for dz in range(2):
            for y in range(1 - dz, height, 2):
                derive_y(2 * t + dz, y)

    def pick(k):
        return v_ref if k == 0 else left.at[k - 1]

    def contract(outer, chunk, ref, lo, hi, base, fresh):
        sites = [
            (chunk * span + dz, y, c)
            for dz in range(span)
            for y in (range(height) if ref is trans_a else range(1 - dz % 2, height, 2))
            for c in range(3)
        ]
        a = jnp.concatenate(
            [ref[z, y if ref is trans_a else y // 2, c, lo:hi] for z, y, c in sites], axis=1
        )
        b = jnp.concatenate(
            [
                jnp.concatenate([pick(outer * 2 + s)[z, y, c] for z, y, c in sites], axis=1)
                for s in range(2)
            ],
            axis=0,
        )
        product = lax.dot_general(
            a, b, (((1,), (1,)), ((), ())), preferred_element_type=jnp.float32
        )
        columns = slice(outer * two, (outer + 1) * two)
        if fresh:
            acc[base + lo : base + hi, columns] = product
        else:
            acc[base + lo : base + hi, columns] += product

    half = 4 * rows

    def contract_all(outer, ref, lo, hi, base):
        contract(outer, 0, ref, lo, hi, base, True)
        pl.loop(1, chunks)(lambda k: contract(outer, k, ref, lo, hi, base, False))

    pl.loop(0, depth)(pass_x)
    far[0].wait()
    relay[0].start()
    pl.loop(0, depth // 2 - 1)(pass_z)
    for copy in z_copies:
        copy.wait()
    rim_z_copy.wait()
    for y in range(1, height, 2):
        put(edge_z, (y,), coefficients(rim_z[y]))
    pass_z_edges()
    near.wait()
    contract_all(0, trans_a, 0, half, 0)
    contract_all(0, trans_b, 0, two, half)
    rim_y_copy.wait()

    @pl.loop(0, depth // 2)
    def _(t):
        put(edge_y, (2 * t + 1,), coefficients(rim_y[2 * t + 1]))

    for copy in y_copies:
        copy.wait()
    pl.loop(0, depth // 2)(pass_y)
    contract_all(0, trans_b, two, half, half)

    left_half = lax.broadcasted_iota(jnp.int32, (1, two), 1) < rows
    kept_near, kept_far = side, pair

    def turn(value):
        return pltpu.roll(value, rows, 1)

    def exchange(stage, phase, step):
        source = outgo[stage].at[member(step)] if phase == 0 else reduced[stage]
        target = income[stage] if phase == 0 else gathered[stage]
        return pltpu.make_async_remote_copy(
            src_ref=source,
            dst_ref=target.at[me_g],
            send_sem=red_sem.at[stage, phase, 0, step],
            recv_sem=red_sem.at[stage, phase, 1, step],
            device_id=place(member(step)),
            device_id_type=MESH,
        )

    def cross(k, phase, step):
        source = cross_out.at[k - 1, member(step)] if phase == 0 else back_out.at[k - 1]
        target = cross_in if phase == 0 else back_in
        return pltpu.make_async_remote_copy(
            src_ref=source,
            dst_ref=target.at[k - 1, me_g],
            send_sem=cross_sem.at[k - 1, phase, 0, step],
            recv_sem=cross_sem.at[k - 1, phase, 1, step],
            device_id=place(member(step), k),
            device_id_type=MESH,
        )

    stage_partners = [(1,), (2, 3)]
    stage_rows = [
        [slot * rows for slot in range(8)],
        [slot * rows for slot in (0, 1, 2, 3, 4, 6)],
    ]

    def prepare(stage):
        columns = slice(stage * two, (stage + 1) * two)
        sent = []
        for op in range(2):
            base = half + op * two
            block = acc[base : base + two, columns]
            turned = jnp.transpose(block)
            if stage == 0:
                own = turned[0:rows]
                acc[base : base + rows, columns] = block[0:rows] - jnp.where(left_half, own, 0.0)
                acc[base + rows : base + two, columns] = block[rows:two] + jnp.where(
                    left_half, turn(own), 0.0
                )
                sent.append([turned[rows:two]])
            else:
                acc[base : base + rows, columns] = jnp.where(
                    kept_far == 0, block[0:rows], block[rows:two]
                )
                sent.append([turned[0:rows], turned[rows:two]])
        kept = kept_near if stage == 0 else kept_far
        for at, k in enumerate(stage_partners[stage]):
            first, second = sent[0][at], sent[1][at]
            if_real = jnp.where(left_half, -first, -turn(second))
            if_imag = jnp.where(left_half, turn(first), second)
            message = jnp.where(kept == 1, if_real, if_imag).astype(jnp.bfloat16)
            for g in range(group):
                cross_out[k - 1, g] = message[g * share : (g + 1) * share]

    def scatter_start(stage):
        columns = slice(stage * two, (stage + 1) * two)
        prepare(stage)
        for g in range(group):
            for at, row in enumerate(stage_rows[stage]):
                outgo[stage][g, at * share : (at + 1) * share] = acc[
                    row + g * share : row + (g + 1) * share, columns
                ].astype(jnp.bfloat16)
        for step in range(1, group):
            exchange(stage, 0, step).start()
        for k in stage_partners[stage]:
            for step in range(group):
                cross(k, 0, step).start()

    def gather_start(stage):
        columns = slice(stage * two, (stage + 1) * two)
        for step in range(1, group):
            exchange(stage, 0, step).wait()
        for k in stage_partners[stage]:
            for step in range(group):
                cross(k, 0, step).wait()
        parts = []
        for at, row in enumerate(stage_rows[stage]):
            if share % 8 == 0:
                mine = pl.ds(pl.multiple_of(row + me_g * share, share), share)
                total = acc[mine, columns]
            else:
                total = outgo[stage][me_g, at * share : (at + 1) * share].astype(jnp.float32)
            for step in range(1, group):
                total = total + income[stage][
                    member(step), at * share : (at + 1) * share
                ].astype(jnp.float32)
            parts.append(total)
        extra = []
        for k in stage_partners[stage]:
            total = cross_in[k - 1, 0].astype(jnp.float32)
            for g in range(1, group):
                total = total + cross_in[k - 1, g].astype(jnp.float32)
            extra.append(total)
        if stage == 0:
            adds = [turn(extra[0]), extra[0]]
            for op in range(2):
                add = jnp.where(left_half, 0.0, adds[op])
                for part in range(2):
                    at = 4 + op * 2 + part
                    parts[at] = parts[at] + jnp.where(kept_near == part, add, 0.0)
            kept_of = [
                jnp.where(kept_near == 0, parts[4 + op * 2], parts[5 + op * 2]) for op in range(2)
            ]
            backs = [jnp.where(left_half, turn(kept_of[0]), kept_of[1])]
        else:
            parts[4] = parts[4] + jnp.where(left_half, extra[0], turn(extra[1]))
            parts[5] = parts[5] + jnp.where(left_half, turn(extra[0]), extra[1])
            backs = [
                jnp.where(left_half, parts[4], turn(parts[5])),
                jnp.where(left_half, turn(parts[4]), parts[5]),
            ]
        for at, total in enumerate(parts):
            rounded = total.astype(jnp.bfloat16)
            reduced[stage][at * share : (at + 1) * share] = rounded
            gathered[stage][me_g, at * share : (at + 1) * share] = rounded
        for k, back in zip(stage_partners[stage], backs):
            back_out[k - 1] = back.astype(jnp.bfloat16)
        for step in range(1, group):
            exchange(stage, 1, step).start()
        for k in stage_partners[stage]:
            for step in range(group):
                cross(k, 1, step).start()

    scale = 1.0 / math.sqrt(width * height * gy_n * depth * gz_n)

    def gather_finish(stage):
        for step in range(1, group):
            exchange(stage, 1, step).wait()
        for k in stage_partners[stage]:
            for step in range(group):
                cross(k, 1, step).wait()

        def slot(at):
            return jnp.concatenate(
                [
                    gathered[stage][g, at * share : (at + 1) * share].astype(jnp.float32)
                    for g in range(group)
                ],
                axis=0,
            )

        ks = stage_partners[stage]
        mirror = jnp.transpose(
            jnp.concatenate(
                [
                    back_in[k - 1, g].astype(jnp.float32)
                    for k in (ks if len(ks) == 2 else ks * 2)
                    for g in range(group)
                ],
                axis=0,
            )
        )
        full = [slot(at) for at in range(4)]
        for op in range(2):
            flipped = mirror[op * rows : (op + 1) * rows]
            for part in range(2):
                other = -flipped if part == 0 else flipped
                if stage == 0:
                    mine = slot(4 + op * 2 + part)
                    full.append(
                        jnp.where(left_half, mine, jnp.where(kept_near == part, mine, other))
                    )
                else:
                    full.append(jnp.where(kept_far == part, slot(4 + op), other))
        full = [jnp.where(side == 0, value, turn(value)) * scale for value in full]
        which = pair if stage == 0 else 1 - pair
        columns = pl.ds(pl.multiple_of(which * two, two), two)
        for part in range(2):
            along_x, phased, along_z, along_y = [full[2 * op + part] for op in range(4)]
            for op in range(3):
                chosen = directions_ref[op]
                out_ref[op * two + part * rows : op * two + (part + 1) * rows, columns] = jnp.where(
                    chosen == 0, along_x, jnp.where(chosen == 1, along_y, along_z)
                )
            out_ref[3 * two + part * rows : 3 * two + (part + 1) * rows, columns] = phased

    scatter_start(0)
    for k in range(chunks + 1):
        if 0 < k < chunks:
            far[k].wait()
            relay[k].start()
        if k == 2:
            gather_start(0)
        if k:
            relay[k - 1].wait()
            contract(1, k - 1, trans_a, 0, half, 0, k == 1)
            contract(1, k - 1, trans_b, 0, half, half, k == 1)
    scatter_start(1)
    gather_finish(0)
    gather_start(1)
    gather_finish(1)


def body(vectors, links, momentum, directions):
    rows, _, depth, height, lanes = vectors.shape
    gz_n = lax.axis_size("gz")
    gy_n = lax.axis_size("gy")
    vec_n = lax.axis_size("vec")
    group = gz_n * gy_n
    assert vec_n == 4 and depth % 2 == 0 and height % 2 == 0 and rows % group == 0
    chunks = split_chunks(depth, 4)
    v = jnp.transpose(vectors, (2, 3, 1, 0, 4))
    packed = jnp.transpose(links, (0, 3, 4, 1, 2, 5)).reshape(3, depth, height, 9, lanes)

    bf16, f32 = jnp.bfloat16, jnp.float32
    share = rows // group
    slots = (8, 6)
    remote_count = 3 + depth + height + 2 * chunks
    vmem = pl.BlockSpec(memory_space=pltpu.VMEM)
    hbm = pl.BlockSpec(memory_space=pltpu.HBM)
    sizes = (gz_n, gy_n, vec_n, depth, height, rows, lanes // 2, chunks)
    parts = [pltpu.VMEM((group, n * share, 2 * rows), bf16) for n in slots]
    small = pltpu.VMEM((3, group, share, 2 * rows), bf16)
    out = pl.pallas_call(
        functools.partial(kernel, sizes),
        out_shape=jax.ShapeDtypeStruct((8 * rows, vec_n * rows), f32),
        in_specs=[hbm, hbm, vmem, vmem],
        out_specs=vmem,
        scratch_shapes=[
            pltpu.VMEM((3, depth, height, 3, rows, lanes), bf16),
            pltpu.VMEM((depth, 3, rows, lanes), bf16),
            pltpu.VMEM((height, 3, rows, lanes), bf16),
            pltpu.VMEM((depth, 9, lanes), bf16),
            pltpu.VMEM((height, 9, lanes), bf16),
            pltpu.VMEM((2, depth, height, 32, lanes), f32),
            pltpu.VMEM((depth, height, 32, lanes), f32),
            pltpu.VMEM((depth, height, 32, lanes), f32),
            pltpu.VMEM((depth, 32, lanes), f32),
            pltpu.VMEM((height, 32, lanes), f32),
            pltpu.VMEM((depth * height, lanes), f32),
            pltpu.VMEM((depth * height, lanes), f32),
            pltpu.VMEM((depth, height, 3, 4 * rows, lanes), bf16),
            pltpu.VMEM((depth, height // 2, 3, 4 * rows, lanes), bf16),
            pltpu.VMEM((8 * rows, vec_n * rows), f32),
            pltpu.SMEM((3,), jnp.int32),
            pltpu.SMEM((3,), jnp.int32),
            parts,
            parts,
            [pltpu.VMEM((n * share, 2 * rows), bf16) for n in slots],
            parts,
            small,
            small,
            pltpu.VMEM((3, share, 2 * rows), bf16),
            small,
            pltpu.SemaphoreType.DMA((2,)),
            pltpu.SemaphoreType.DMA((remote_count,)),
            pltpu.SemaphoreType.DMA((remote_count,)),
            pltpu.SemaphoreType.DMA((2, 2, 2, group)),
            pltpu.SemaphoreType.DMA((3, 2, 2, group)),
        ],
        compiler_params=pltpu.CompilerParams(
            collective_id=0, has_side_effects=True, vmem_limit_bytes=48 * 1024 * 1024
        ),
    )(momentum, directions, v, packed)
    return out.reshape(4, 2, rows, vec_n * rows)


def solution(mesh):
    in_specs = (P("vec", None, "gz", "gy", None), P(None, None, None, "gz", "gy", None), P(), P())
    out_specs = P(None, None, "vec", None)
    return jax.shard_map(body, mesh=mesh, in_specs=in_specs, out_specs=out_specs, check_vma=False)
```

```python
import functools
import math

import jax
import jax.numpy as jnp
from jax import lax
from jax.experimental import pallas as pl
from jax.experimental.pallas import tpu as pltpu
from jax.sharding import PartitionSpec as P

MESH = pl.DeviceIdType.MESH


def split_chunks(depth, most):
    count = most
    while depth % count or (depth // count) % 2:
        count -= 1
    return count


def kernel(
    sizes,
    momentum_in,
    directions_in,
    v_ref,
    links_ref,
    out_ref,
    left,
    halo_y,
    halo_z,
    rim_y,
    rim_z,
    tab_x,
    tab_y,
    tab_z,
    edge_y,
    edge_z,
    cos_ref,
    sin_ref,
    trans_a,
    trans_b,
    acc,
    momentum_ref,
    directions_ref,
    outgo,
    income,
    reduced,
    gathered,
    cross_out,
    cross_in,
    back_out,
    back_in,
    local_sem,
    send_sem,
    recv_sem,
    red_sem,
    cross_sem,
    greet_sem,
):
    gz_n, gy_n, vec_n, depth, height, rows, width, chunks = sizes
    lanes = 2 * width
    two = 2 * rows
    me_z = lax.axis_index("gz")
    me_y = lax.axis_index("gy")
    me_v = lax.axis_index("vec")
    pair = me_v // 2
    side = lax.rem(me_v, 2)
    group = gz_n * gy_n
    me_g = me_z * gy_n + me_y
    span = depth // chunks
    share = rows // group
    partners = [me_v, pair * 2 + 1 - side, (1 - pair) * 2 + side, (1 - pair) * 2 + 1 - side]

    def member(step):
        return lax.rem(me_g + step, group)

    def place(g, k=0):
        return {"gz": g // gy_n, "gy": lax.rem(g, gy_n), "vec": partners[k]}

    z_up = {"gz": lax.rem(me_z + 1, gz_n)}
    z_down = {"gz": lax.rem(me_z + gz_n - 1, gz_n)}
    y_up = {"gy": lax.rem(me_y + 1, gy_n)}
    y_down = {"gy": lax.rem(me_y + gy_n - 1, gy_n)}
    sibling = {"vec": partners[1]}
    across = {"vec": partners[2]}
    y_sides = [y_up] if gy_n == 2 else [y_up, y_down]

    def tell(sem, device):
        pl.semaphore_signal(sem, inc=1, device_id=device, device_id_type=MESH)

    def tell_z(sem):
        pl.when(me_z > 0)(lambda: tell(sem, z_down))
        pl.when(me_z < gz_n - 1)(lambda: tell(sem, z_up))

    z_sides = jnp.where(me_z > 0, 1, 0) + jnp.where(me_z < gz_n - 1, 1, 0)
    barrier = pltpu.get_barrier_semaphore()
    for device in [sibling, across] + y_sides:
        tell(barrier, device)
    tell_z(barrier)

    def greet(number):
        sem = greet_sem.at[number]
        if number == 0:
            tell(sem, sibling)
        elif number <= gy_n // 2:
            for device in y_sides:
                tell(sem, device)
        else:
            tell_z(sem)

    def heard(number):
        sides = 1 if number == 0 else len(y_sides) if number <= gy_n // 2 else z_sides
        pl.semaphore_wait(greet_sem.at[number], sides)

    rounds = gy_n // 2 + gz_n
    scalars = [
        pltpu.make_async_copy(momentum_in, momentum_ref, local_sem.at[0]),
        pltpu.make_async_copy(directions_in, directions_ref, local_sem.at[1]),
    ]
    for copy in scalars:
        copy.start()

    lane = lax.broadcasted_iota(jnp.int32, (1, lanes), 1)
    low_half = lane < width
    last_mask = lax.rem(lane, width) == width - 1
    first_mask = lax.rem(lane, width) == 0
    sign = jnp.where(low_half, 1.0, -1.0).astype(jnp.float32)
    tile = 32 if rows % 32 == 0 else rows

    def coefficients(raw):
        value = raw.astype(jnp.float32) * 0.5
        swapped = pltpu.roll(value, width, 1)
        real = jnp.where(low_half, value, swapped)
        imag = jnp.where(low_half, -swapped, value)
        return real, imag

    def put(table, where, pair_of):
        table[where + (slice(0, 9),)] = pair_of[0]
        table[where + (slice(16, 25),)] = pair_of[1]

    def step_back(value):
        one = pltpu.roll(value, 1, 1)
        other = pltpu.roll(value, width + 1, 1)
        return jnp.where(first_mask, other, one)

    @pl.loop(0, depth)
    def _(z):
        for y in range(height):
            real, imag = coefficients(links_ref[0, z, y])
            put(tab_x, (0, z, y), (real, imag))
            put(tab_x, (1, z, y), (step_back(real), step_back(imag)))
            put(tab_y, (z, y), coefficients(links_ref[1, z, y]))
            put(tab_z, (z, y), coefficients(links_ref[2, z, y]))

    for copy in scalars:
        copy.wait()
    site_shape = (depth * height, lanes)
    site = lax.broadcasted_iota(jnp.int32, site_shape, 0)
    x_at = lax.rem(lax.broadcasted_iota(jnp.int32, site_shape, 1), width)
    y_at = me_y * height + lax.rem(site, height)
    z_at = me_z * depth + site // height

    def fraction(component, at, extent):
        turned = lax.rem(momentum_ref[component] * at, extent)
        turned = jnp.where(turned < 0, turned + extent, turned)
        return turned.astype(jnp.float32) / extent

    angle = (2.0 * math.pi) * (
        fraction(2, z_at, depth * gz_n)
        + fraction(1, y_at, height * gy_n)
        + fraction(0, x_at, width)
    )
    cos_ref[...] = jnp.cos(angle)
    sin_ref[...] = jnp.sin(angle) * sign

    pl.semaphore_wait(barrier, 2 + len(y_sides) + z_sides)

    counter = [0]

    def remote(src, dst, device):
        index = counter[0]
        counter[0] += 1
        return pltpu.make_async_remote_copy(
            src_ref=src,
            dst_ref=dst,
            send_sem=send_sem.at[index],
            recv_sem=recv_sem.at[index],
            device_id=device,
            device_id_type=MESH,
        )

    rim_y_copy = remote(links_ref.at[1, :, height - 1], rim_y, y_up)
    rim_z_copy = remote(links_ref.at[2, depth - 1], rim_z, z_up)
    z_copies = [
        remote(v_ref.at[depth - 1 if y % 2 else 0, y], halo_z.at[y], z_up if y % 2 else z_down)
        for y in range(height)
    ]
    y_copies = [
        remote(v_ref.at[z, height - 1 if z % 2 else 0], halo_y.at[z], y_up if z % 2 else y_down)
        for z in range(depth)
    ]
    near = remote(v_ref, left.at[0], sibling)
    far, relay = [], []
    for k in range(chunks):
        part = pl.ds(k * span, span)
        far.append(remote(v_ref.at[part], left.at[1, part], across))
        relay.append(remote(left.at[1, part], left.at[2, part], sibling))
    far[0].start()
    rim_y_copy.start()
    for copy in y_copies + far[1:]:
        copy.start()
    near.start()

    def store(ref, where, slot, lo, value):
        turned = pltpu.roll(value, width, 1) * sign
        ref[where + (pl.ds(slot * two + lo, tile),)] = value.astype(jnp.bfloat16)
        ref[where + (pl.ds(slot * two + rows + lo, tile),)] = turned.astype(jnp.bfloat16)

    def load(z, y, colour, lo):
        return v_ref[z, y, colour, pl.ds(lo, tile)].astype(jnp.float32)

    def stencil(ref, where, lo, slot, ahead, behind, up, down):
        sums = [0.0, 0.0, 0.0]
        for col in range(3):
            value, swapped = ahead(col)
            for row in range(3):
                k = row * 3 + col
                sums[row] = sums[row] + (up(k) * value + up(16 + k) * swapped)
        for col in range(3):
            value, swapped = behind(col)
            for row in range(3):
                k = col * 3 + row
                sums[row] = sums[row] + (down(16 + k) * swapped - down(k) * value)
        for row in range(3):
            store(ref, where + (row,), slot, lo, sums[row])

    def swap(value):
        return value, pltpu.roll(value, width, 1)

    def pass_x(z):
        for y in range(height):
            for lo in range(0, rows, tile):
                here = pl.ds(z * height + y, 1)
                cosine = cos_ref[here]
                sine = sin_ref[here]

                def ahead(col):
                    value = load(z, y, col, lo)
                    one = pltpu.roll(value, lanes - 1, 1)
                    other = pltpu.roll(value, width - 1, 1)
                    return jnp.where(last_mask, other, one), jnp.where(last_mask, one, other)

                def behind(col):
                    value = load(z, y, col, lo)
                    one = pltpu.roll(value, 1, 1)
                    other = pltpu.roll(value, width + 1, 1)
                    return jnp.where(first_mask, other, one), jnp.where(first_mask, one, other)

                stencil(
                    trans_a, (z, y), lo, 0, ahead, behind,
                    lambda k: tab_x[0, z, y, k : k + 1],
                    lambda k: tab_x[1, z, y, k : k + 1],
                )
                for col in range(3):
                    value, swapped = swap(load(z, y, col, lo))
                    store(trans_a, (z, y, col), 1, lo, value * cosine + swapped * sine)

    def halo(ref, at):
        return lambda col, lo: ref[at, col, pl.ds(lo, tile)].astype(jnp.float32)

    def inside(z, y):
        return lambda col, lo: load(z, y, col, lo)

    def derive(z, y, slot, ahead, behind, up, down):
        for lo in range(0, rows, tile):
            stencil(
                trans_b, (z, y // 2), lo, slot,
                lambda col: swap(ahead(col, lo)),
                lambda col: swap(behind(col, lo)),
                up,
                down,
            )

    def table(ref, where):
        return lambda k: ref[where + (slice(k, k + 1),)]

    def derive_z(z, y, ahead=None, behind=None, down=None):
        derive(
            z, y, 0,
            ahead or inside(z + 1, y),
            behind or inside(z - 1, y),
            table(tab_z, (z, y)),
            down or table(tab_z, (z - 1, y)),
        )

    def derive_y(z, y):
        top, bottom = y == height - 1, y == 0
        derive(
            z, y, 1,
            halo(halo_y, z) if top else inside(z, y + 1),
            halo(halo_y, z) if bottom else inside(z, y - 1),
            table(tab_y, (z, y)),
            table(edge_y, (z,)) if bottom else table(tab_y, (z, y - 1)),
        )

    def pass_z(t):
        for y in range(0, height, 2):
            derive_z(2 * t + 1, y)
        for y in range(1, height, 2):
            derive_z(2 * t + 2, y)

    def pass_z_edges():
        for y in range(1, height, 2):
            derive_z(0, y, behind=halo(halo_z, y), down=table(edge_z, (y,)))
        for y in range(0, height, 2):
            derive_z(depth - 1, y, ahead=halo(halo_z, y))

    def pass_y(t):
        for dz in range(2):
            for y in range(1 - dz, height, 2):
                derive_y(2 * t + dz, y)

    def pick(k):
        return v_ref if k == 0 else left.at[k - 1]

    def contract(outer, chunk, ref, lo, hi, base, fresh):
        sites = [
            (chunk * span + dz, y, c)
            for dz in range(span)
            for y in (range(height) if ref is trans_a else range(1 - dz % 2, height, 2))
            for c in range(3)
        ]
        a = jnp.concatenate(
            [ref[z, y if ref is trans_a else y // 2, c, lo:hi] for z, y, c in sites], axis=1
        )
        b = jnp.concatenate(
            [
                jnp.concatenate([pick(outer * 2 + s)[z, y, c] for z, y, c in sites], axis=1)
                for s in range(2)
            ],
            axis=0,
        )
        product = lax.dot_general(
            a, b, (((1,), (1,)), ((), ())), preferred_element_type=jnp.float32
        )
        columns = slice(outer * two, (outer + 1) * two)
        if fresh:
            acc[base + lo : base + hi, columns] = product
        else:
            acc[base + lo : base + hi, columns] += product

    half = 4 * rows

    def contract_all(outer, ref, lo, hi, base):
        contract(outer, 0, ref, lo, hi, base, True)
        pl.loop(1, chunks)(lambda k: contract(outer, k, ref, lo, hi, base, False))

    def turn_round(number):
        if number:
            heard(number - 1)
        greet(number)

    early = min(rounds, depth // 2)

    @pl.loop(0, depth)
    def _(z):
        for number in range(early):
            pl.when(z == 2 * number)(functools.partial(turn_round, number))
        pass_x(z)

    for number in range(early, rounds):
        turn_round(number)
    far[0].wait()
    relay[0].start()
    pl.loop(0, depth // 2 - 1)(pass_z)
    heard(rounds - 1)
    rim_z_copy.start()
    for copy in z_copies:
        copy.start()
    near.wait()
    contract_all(0, trans_a, 0, half, 0)
    rim_y_copy.wait()

    @pl.loop(0, depth // 2)
    def _(t):
        put(edge_y, (2 * t + 1,), coefficients(rim_y[2 * t + 1]))

    for copy in y_copies:
        copy.wait()
    pl.loop(0, depth // 2)(pass_y)
    far[1].wait()
    relay[1].start()
    rim_z_copy.wait()
    for copy in z_copies:
        copy.wait()
    for y in range(1, height, 2):
        put(edge_z, (y,), coefficients(rim_z[y]))
    pass_z_edges()
    contract_all(0, trans_b, 0, half, half)

    left_half = lax.broadcasted_iota(jnp.int32, (1, two), 1) < rows
    kept_near, kept_far = side, pair

    def turn(value):
        return pltpu.roll(value, rows, 1)

    def exchange(stage, phase, step):
        source = outgo[stage].at[member(step)] if phase == 0 else reduced[stage]
        target = income[stage] if phase == 0 else gathered[stage]
        return pltpu.make_async_remote_copy(
            src_ref=source,
            dst_ref=target.at[me_g],
            send_sem=red_sem.at[stage, phase, 0, step],
            recv_sem=red_sem.at[stage, phase, 1, step],
            device_id=place(member(step)),
            device_id_type=MESH,
        )

    def cross(k, phase, step):
        source = cross_out.at[k - 1, member(step)] if phase == 0 else back_out.at[k - 1]
        target = cross_in if phase == 0 else back_in
        return pltpu.make_async_remote_copy(
            src_ref=source,
            dst_ref=target.at[k - 1, me_g],
            send_sem=cross_sem.at[k - 1, phase, 0, step],
            recv_sem=cross_sem.at[k - 1, phase, 1, step],
            device_id=place(member(step), k),
            device_id_type=MESH,
        )

    stage_partners = [(1,), (2, 3)]
    stage_rows = [
        [slot * rows for slot in range(8)],
        [slot * rows for slot in (0, 1, 2, 3, 4, 6)],
    ]

    def prepare(stage):
        columns = slice(stage * two, (stage + 1) * two)
        sent = []
        for op in range(2):
            base = half + op * two
            block = acc[base : base + two, columns]
            turned = jnp.transpose(block)
            if stage == 0:
                own = turned[0:rows]
                acc[base : base + rows, columns] = block[0:rows] - jnp.where(left_half, own, 0.0)
                acc[base + rows : base + two, columns] = block[rows:two] + jnp.where(
                    left_half, turn(own), 0.0
                )
                sent.append([turned[rows:two]])
            else:
                acc[base : base + rows, columns] = jnp.where(
                    kept_far == 0, block[0:rows], block[rows:two]
                )
                sent.append([turned[0:rows], turned[rows:two]])
        kept = kept_near if stage == 0 else kept_far
        for at, k in enumerate(stage_partners[stage]):
            first, second = sent[0][at], sent[1][at]
            if_real = jnp.where(left_half, -first, -turn(second))
            if_imag = jnp.where(left_half, turn(first), second)
            message = jnp.where(kept == 1, if_real, if_imag).astype(jnp.bfloat16)
            for g in range(group):
                cross_out[k - 1, g] = message[g * share : (g + 1) * share]

    def scatter_start(stage):
        columns = slice(stage * two, (stage + 1) * two)
        prepare(stage)
        for g in range(group):
            for at, row in enumerate(stage_rows[stage]):
                outgo[stage][g, at * share : (at + 1) * share] = acc[
                    row + g * share : row + (g + 1) * share, columns
                ].astype(jnp.bfloat16)
        for step in range(1, group):
            exchange(stage, 0, step).start()
        for k in stage_partners[stage]:
            for step in range(group):
                cross(k, 0, step).start()

    def gather_start(stage):
        columns = slice(stage * two, (stage + 1) * two)
        for step in range(1, group):
            exchange(stage, 0, step).wait()
        for k in stage_partners[stage]:
            for step in range(group):
                cross(k, 0, step).wait()
        parts = []
        for at, row in enumerate(stage_rows[stage]):
            if share % 8 == 0:
                mine = pl.ds(pl.multiple_of(row + me_g * share, share), share)
                total = acc[mine, columns]
            else:
                total = outgo[stage][me_g, at * share : (at + 1) * share].astype(jnp.float32)
            for step in range(1, group):
                total = total + income[stage][
                    member(step), at * share : (at + 1) * share
                ].astype(jnp.float32)
            parts.append(total)
        extra = []
        for k in stage_partners[stage]:
            total = cross_in[k - 1, 0].astype(jnp.float32)
            for g in range(1, group):
                total = total + cross_in[k - 1, g].astype(jnp.float32)
            extra.append(total)
        if stage == 0:
            adds = [turn(extra[0]), extra[0]]
            for op in range(2):
                add = jnp.where(left_half, 0.0, adds[op])
                for part in range(2):
                    at = 4 + op * 2 + part
                    parts[at] = parts[at] + jnp.where(kept_near == part, add, 0.0)
            kept_of = [
                jnp.where(kept_near == 0, parts[4 + op * 2], parts[5 + op * 2]) for op in range(2)
            ]
            backs = [jnp.where(left_half, turn(kept_of[0]), kept_of[1])]
        else:
            parts[4] = parts[4] + jnp.where(left_half, extra[0], turn(extra[1]))
            parts[5] = parts[5] + jnp.where(left_half, turn(extra[0]), extra[1])
            backs = [
                jnp.where(left_half, parts[4], turn(parts[5])),
                jnp.where(left_half, turn(parts[4]), parts[5]),
            ]
        for at, total in enumerate(parts):
            rounded = total.astype(jnp.bfloat16)
            reduced[stage][at * share : (at + 1) * share] = rounded
            gathered[stage][me_g, at * share : (at + 1) * share] = rounded
        for k, back in zip(stage_partners[stage], backs):
            back_out[k - 1] = back.astype(jnp.bfloat16)
        for step in range(1, group):
            exchange(stage, 1, step).start()
        for k in stage_partners[stage]:
            for step in range(group):
                cross(k, 1, step).start()

    scale = 1.0 / math.sqrt(width * height * gy_n * depth * gz_n)

    def gather_finish(stage):
        for step in range(1, group):
            exchange(stage, 1, step).wait()
        for k in stage_partners[stage]:
            for step in range(group):
                cross(k, 1, step).wait()

        def slot(at):
            return jnp.concatenate(
                [
                    gathered[stage][g, at * share : (at + 1) * share].astype(jnp.float32)
                    for g in range(group)
                ],
                axis=0,
            )

        ks = stage_partners[stage]
        mirror = jnp.transpose(
            jnp.concatenate(
                [
                    back_in[k - 1, g].astype(jnp.float32)
                    for k in (ks if len(ks) == 2 else ks * 2)
                    for g in range(group)
                ],
                axis=0,
            )
        )
        full = [slot(at) for at in range(4)]
        for op in range(2):
            flipped = mirror[op * rows : (op + 1) * rows]
            for part in range(2):
                other = -flipped if part == 0 else flipped
                if stage == 0:
                    mine = slot(4 + op * 2 + part)
                    full.append(
                        jnp.where(left_half, mine, jnp.where(kept_near == part, mine, other))
                    )
                else:
                    full.append(jnp.where(kept_far == part, slot(4 + op), other))
        full = [jnp.where(side == 0, value, turn(value)) * scale for value in full]
        which = pair if stage == 0 else 1 - pair
        columns = pl.ds(pl.multiple_of(which * two, two), two)
        for part in range(2):
            along_x, phased, along_z, along_y = [full[2 * op + part] for op in range(4)]
            for op in range(3):
                chosen = directions_ref[op]
                out_ref[op * two + part * rows : op * two + (part + 1) * rows, columns] = jnp.where(
                    chosen == 0, along_x, jnp.where(chosen == 1, along_y, along_z)
                )
            out_ref[3 * two + part * rows : 3 * two + (part + 1) * rows, columns] = phased

    scatter_start(0)
    for k in range(2, chunks + 2):
        if k < chunks:
            far[k].wait()
            relay[k].start()
        relay[k - 2].wait()
        contract(1, k - 2, trans_a, 0, half, 0, k == 2)
        contract(1, k - 2, trans_b, 0, half, half, k == 2)
    scatter_start(1)
    gather_start(0)
    gather_start(1)
    gather_finish(0)
    gather_finish(1)


def body(vectors, links, momentum, directions):
    rows, _, depth, height, lanes = vectors.shape
    gz_n = lax.axis_size("gz")
    gy_n = lax.axis_size("gy")
    vec_n = lax.axis_size("vec")
    group = gz_n * gy_n
    assert vec_n == 4 and depth % 2 == 0 and height % 2 == 0 and rows % group == 0
    chunks = split_chunks(depth, 4)
    v = jnp.transpose(vectors, (2, 3, 1, 0, 4))
    packed = jnp.transpose(links, (0, 3, 4, 1, 2, 5)).reshape(3, depth, height, 9, lanes)

    bf16, f32 = jnp.bfloat16, jnp.float32
    share = rows // group
    slots = (8, 6)
    remote_count = 3 + depth + height + 2 * chunks
    vmem = pl.BlockSpec(memory_space=pltpu.VMEM)
    hbm = pl.BlockSpec(memory_space=pltpu.HBM)
    sizes = (gz_n, gy_n, vec_n, depth, height, rows, lanes // 2, chunks)
    parts = [pltpu.VMEM((group, n * share, 2 * rows), bf16) for n in slots]
    small = pltpu.VMEM((3, group, share, 2 * rows), bf16)
    out = pl.pallas_call(
        functools.partial(kernel, sizes),
        out_shape=jax.ShapeDtypeStruct((8 * rows, vec_n * rows), f32),
        in_specs=[hbm, hbm, vmem, vmem],
        out_specs=vmem,
        scratch_shapes=[
            pltpu.VMEM((3, depth, height, 3, rows, lanes), bf16),
            pltpu.VMEM((depth, 3, rows, lanes), bf16),
            pltpu.VMEM((height, 3, rows, lanes), bf16),
            pltpu.VMEM((depth, 9, lanes), bf16),
            pltpu.VMEM((height, 9, lanes), bf16),
            pltpu.VMEM((2, depth, height, 32, lanes), f32),
            pltpu.VMEM((depth, height, 32, lanes), f32),
            pltpu.VMEM((depth, height, 32, lanes), f32),
            pltpu.VMEM((depth, 32, lanes), f32),
            pltpu.VMEM((height, 32, lanes), f32),
            pltpu.VMEM((depth * height, lanes), f32),
            pltpu.VMEM((depth * height, lanes), f32),
            pltpu.VMEM((depth, height, 3, 4 * rows, lanes), bf16),
            pltpu.VMEM((depth, height // 2, 3, 4 * rows, lanes), bf16),
            pltpu.VMEM((8 * rows, vec_n * rows), f32),
            pltpu.SMEM((3,), jnp.int32),
            pltpu.SMEM((3,), jnp.int32),
            parts,
            parts,
            [pltpu.VMEM((n * share, 2 * rows), bf16) for n in slots],
            parts,
            small,
            small,
            pltpu.VMEM((3, share, 2 * rows), bf16),
            small,
            pltpu.SemaphoreType.DMA((2,)),
            pltpu.SemaphoreType.DMA((remote_count,)),
            pltpu.SemaphoreType.DMA((remote_count,)),
            pltpu.SemaphoreType.DMA((2, 2, 2, group)),
            pltpu.SemaphoreType.DMA((3, 2, 2, group)),
            pltpu.SemaphoreType.REGULAR((gy_n // 2 + gz_n,)),
        ],
        compiler_params=pltpu.CompilerParams(
            collective_id=0, has_side_effects=True, vmem_limit_bytes=48 * 1024 * 1024
        ),
    )(momentum, directions, v, packed)
    return out.reshape(4, 2, rows, vec_n * rows)


def solution(mesh):
    in_specs = (P("vec", None, "gz", "gy", None), P(None, None, None, "gz", "gy", None), P(), P())
    out_specs = P(None, None, "vec", None)
    return jax.shard_map(body, mesh=mesh, in_specs=in_specs, out_specs=out_specs, check_vma=False)
```

```python
import functools
import math

import jax
import jax.numpy as jnp
from jax import lax
from jax.experimental import pallas as pl
from jax.experimental.pallas import tpu as pltpu
from jax.sharding import PartitionSpec as P

MESH = pl.DeviceIdType.MESH


def split_chunks(depth, most):
    count = most
    while depth % count or (depth // count) % 2:
        count -= 1
    return count


def kernel(
    sizes,
    momentum_in,
    directions_in,
    v_ref,
    links_ref,
    out_ref,
    left,
    halo_y,
    halo_z,
    rim_y,
    rim_z,
    tab_x,
    tab_y,
    tab_z,
    edge_y,
    edge_z,
    cos_ref,
    sin_ref,
    trans_a,
    trans_b,
    trans_c,
    acc,
    acc_c,
    momentum_ref,
    directions_ref,
    outgo,
    income,
    reduced,
    gathered,
    cross_out,
    cross_in,
    back_out,
    back_in,
    local_sem,
    send_sem,
    recv_sem,
    red_sem,
    cross_sem,
    greet_sem,
):
    gz_n, gy_n, vec_n, depth, height, rows, width, chunks = sizes
    lanes = 2 * width
    two = 2 * rows
    me_z = lax.axis_index("gz")
    me_y = lax.axis_index("gy")
    me_v = lax.axis_index("vec")
    pair = me_v // 2
    side = lax.rem(me_v, 2)
    group = gz_n * gy_n
    me_g = me_z * gy_n + me_y
    span = depth // chunks
    share = rows // group
    partners = [me_v, pair * 2 + 1 - side, (1 - pair) * 2 + side, (1 - pair) * 2 + 1 - side]

    def member(step):
        return lax.rem(me_g + step, group)

    def place(g, k=0):
        return {"gz": g // gy_n, "gy": lax.rem(g, gy_n), "vec": partners[k]}

    z_up = {"gz": lax.rem(me_z + 1, gz_n)}
    z_down = {"gz": lax.rem(me_z + gz_n - 1, gz_n)}
    y_up = {"gy": lax.rem(me_y + 1, gy_n)}
    y_down = {"gy": lax.rem(me_y + gy_n - 1, gy_n)}
    sibling = {"vec": partners[1]}
    across = {"vec": partners[2]}
    y_sides = [y_up] if gy_n == 2 else [y_up, y_down]

    def tell(sem, device):
        pl.semaphore_signal(sem, inc=1, device_id=device, device_id_type=MESH)

    def tell_z(sem):
        pl.when(me_z > 0)(lambda: tell(sem, z_down))
        pl.when(me_z < gz_n - 1)(lambda: tell(sem, z_up))

    z_sides = jnp.where(me_z > 0, 1, 0) + jnp.where(me_z < gz_n - 1, 1, 0)
    barrier = pltpu.get_barrier_semaphore()
    for device in [sibling, across] + y_sides:
        tell(barrier, device)
    tell_z(barrier)

    def greet(number):
        sem = greet_sem.at[number]
        if number == 0:
            tell(sem, sibling)
        elif number <= gy_n // 2:
            for device in y_sides:
                tell(sem, device)
        else:
            tell_z(sem)

    def heard(number):
        sides = 1 if number == 0 else len(y_sides) if number <= gy_n // 2 else z_sides
        pl.semaphore_wait(greet_sem.at[number], sides)

    rounds = gy_n // 2 + gz_n
    scalars = [
        pltpu.make_async_copy(momentum_in, momentum_ref, local_sem.at[0]),
        pltpu.make_async_copy(directions_in, directions_ref, local_sem.at[1]),
    ]
    for copy in scalars:
        copy.start()

    lane = lax.broadcasted_iota(jnp.int32, (1, lanes), 1)
    low_half = lane < width
    last_mask = lax.rem(lane, width) == width - 1
    first_mask = lax.rem(lane, width) == 0
    sign = jnp.where(low_half, 1.0, -1.0).astype(jnp.float32)
    tile = 32 if rows % 32 == 0 else rows

    def coefficients(raw):
        value = raw.astype(jnp.float32) * 0.5
        swapped = pltpu.roll(value, width, 1)
        real = jnp.where(low_half, value, swapped)
        imag = jnp.where(low_half, -swapped, value)
        return real, imag

    def put(table, where, pair_of):
        table[where + (slice(0, 9),)] = pair_of[0]
        table[where + (slice(16, 25),)] = pair_of[1]

    def step_back(value):
        one = pltpu.roll(value, 1, 1)
        other = pltpu.roll(value, width + 1, 1)
        return jnp.where(first_mask, other, one)

    @pl.loop(0, depth)
    def _(z):
        for y in range(height):
            real, imag = coefficients(links_ref[0, z, y])
            put(tab_x, (0, z, y), (real, imag))
            put(tab_x, (1, z, y), (step_back(real), step_back(imag)))
            put(tab_y, (z, y), coefficients(links_ref[1, z, y]))
            put(tab_z, (z, y), coefficients(links_ref[2, z, y]))

    for copy in scalars:
        copy.wait()
    site_shape = (depth * height, lanes)
    site = lax.broadcasted_iota(jnp.int32, site_shape, 0)
    x_at = lax.rem(lax.broadcasted_iota(jnp.int32, site_shape, 1), width)
    y_at = me_y * height + lax.rem(site, height)
    z_at = me_z * depth + site // height

    def fraction(component, at, extent):
        turned = lax.rem(momentum_ref[component] * at, extent)
        turned = jnp.where(turned < 0, turned + extent, turned)
        return turned.astype(jnp.float32) / extent

    angle = (2.0 * math.pi) * (
        fraction(2, z_at, depth * gz_n)
        + fraction(1, y_at, height * gy_n)
        + fraction(0, x_at, width)
    )
    cos_ref[...] = jnp.cos(angle)
    sin_ref[...] = jnp.sin(angle) * sign

    pl.semaphore_wait(barrier, 2 + len(y_sides) + z_sides)

    counter = [0]

    def remote(src, dst, device):
        index = counter[0]
        counter[0] += 1
        return pltpu.make_async_remote_copy(
            src_ref=src,
            dst_ref=dst,
            send_sem=send_sem.at[index],
            recv_sem=recv_sem.at[index],
            device_id=device,
            device_id_type=MESH,
        )

    rim_y_copy = remote(links_ref.at[1, :, height - 1], rim_y, y_up)
    rim_z_copy = remote(links_ref.at[2, depth - 1], rim_z, z_up)
    z_copies = [
        remote(v_ref.at[depth - 1 if y % 2 else 0, y], halo_z.at[y], z_up if y % 2 else z_down)
        for y in range(height)
    ]
    y_copies = [
        remote(v_ref.at[z, height - 1 if z % 2 else 0], halo_y.at[z], y_up if z % 2 else y_down)
        for z in range(depth)
    ]
    near = remote(v_ref, left.at[0], sibling)
    stretch = chunks // 2

    def chunk_at(step, owner):
        return owner * stretch + step if step < stretch else (1 - owner) * stretch + step - stretch

    def pieces(step, owner):
        first = chunk_at(step, owner) * span
        if step < stretch:
            return [(pl.ds(first, span),)]
        return [(first + dz, y) for dz in range(span) for y in range(1 - dz % 2, height, 2)]

    class Copies:
        def __init__(self, copies):
            self.copies = copies

        def start(self):
            for copy in self.copies:
                copy.start()

        def wait(self):
            for copy in self.copies:
                copy.wait()

    far, relay = [], []
    for step in range(chunks):
        far.append(
            Copies(
                [remote(v_ref.at[at], left.at[(1,) + at], across) for at in pieces(step, 1 - pair)]
            )
        )
        relay.append(
            Copies(
                [
                    remote(left.at[(1,) + at], left.at[(2,) + at], sibling)
                    for at in pieces(step, pair)
                ]
            )
        )
    far[0].start()
    rim_y_copy.start()
    for copy in y_copies + far[1:]:
        copy.start()
    near.start()

    def store(ref, where, slot, lo, value):
        turned = pltpu.roll(value, width, 1) * sign
        ref[where + (pl.ds(slot * two + lo, tile),)] = value.astype(jnp.bfloat16)
        ref[where + (pl.ds(slot * two + rows + lo, tile),)] = turned.astype(jnp.bfloat16)

    def load(z, y, colour, lo):
        return v_ref[z, y, colour, pl.ds(lo, tile)].astype(jnp.float32)

    def stencil(ref, where, lo, slot, ahead, behind, up, down):
        sums = [0.0, 0.0, 0.0]
        for col in range(3):
            value, swapped = ahead(col)
            for row in range(3):
                k = row * 3 + col
                sums[row] = sums[row] + (up(k) * value + up(16 + k) * swapped)
        for col in range(3):
            value, swapped = behind(col)
            for row in range(3):
                k = col * 3 + row
                sums[row] = sums[row] + (down(16 + k) * swapped - down(k) * value)
        for row in range(3):
            store(ref, where + (row,), slot, lo, sums[row])

    def swap(value):
        return value, pltpu.roll(value, width, 1)

    def pass_x(z):
        for y in range(height):
            for lo in range(0, rows, tile):
                here = pl.ds(z * height + y, 1)
                cosine = cos_ref[here]
                sine = sin_ref[here]

                def ahead(col):
                    value = load(z, y, col, lo)
                    one = pltpu.roll(value, lanes - 1, 1)
                    other = pltpu.roll(value, width - 1, 1)
                    return jnp.where(last_mask, other, one), jnp.where(last_mask, one, other)

                def behind(col):
                    value = load(z, y, col, lo)
                    one = pltpu.roll(value, 1, 1)
                    other = pltpu.roll(value, width + 1, 1)
                    return jnp.where(first_mask, other, one), jnp.where(first_mask, one, other)

                stencil(
                    trans_a, (z, y), lo, 0, ahead, behind,
                    lambda k: tab_x[0, z, y, k : k + 1],
                    lambda k: tab_x[1, z, y, k : k + 1],
                )
                for col in range(3):
                    value, swapped = swap(load(z, y, col, lo))
                    store(trans_a, (z, y, col), 1, lo, value * cosine + swapped * sine)

    def pass_conjugate(t):
        for dz in range(2):
            for y in range(dz, height, 2):
                z = pair * (depth // 2) + 2 * t + dz
                for lo in range(0, rows, tile):
                    here = pl.ds(z * height + y, 1)
                    cosine = cos_ref[here]
                    sine = sin_ref[here]
                    for col in range(3):
                        value, swapped = swap(load(z, y, col, lo))
                        store(
                            trans_c, (2 * t + dz, y // 2, col), 0, lo,
                            value * cosine - swapped * sine,
                        )

    def halo(ref, at):
        return lambda col, lo: ref[at, col, pl.ds(lo, tile)].astype(jnp.float32)

    def inside(z, y):
        return lambda col, lo: load(z, y, col, lo)

    def derive(z, y, slot, ahead, behind, up, down):
        for lo in range(0, rows, tile):
            stencil(
                trans_b, (z, y // 2), lo, slot,
                lambda col: swap(ahead(col, lo)),
                lambda col: swap(behind(col, lo)),
                up,
                down,
            )

    def table(ref, where):
        return lambda k: ref[where + (slice(k, k + 1),)]

    def derive_z(z, y, ahead=None, behind=None, down=None):
        derive(
            z, y, 0,
            ahead or inside(z + 1, y),
            behind or inside(z - 1, y),
            table(tab_z, (z, y)),
            down or table(tab_z, (z - 1, y)),
        )

    def derive_y(z, y):
        top, bottom = y == height - 1, y == 0
        derive(
            z, y, 1,
            halo(halo_y, z) if top else inside(z, y + 1),
            halo(halo_y, z) if bottom else inside(z, y - 1),
            table(tab_y, (z, y)),
            table(edge_y, (z,)) if bottom else table(tab_y, (z, y - 1)),
        )

    def pass_z(t):
        for y in range(0, height, 2):
            derive_z(2 * t + 1, y)
        for y in range(1, height, 2):
            derive_z(2 * t + 2, y)

    def pass_z_edges():
        for y in range(1, height, 2):
            derive_z(0, y, behind=halo(halo_z, y), down=table(edge_z, (y,)))
        for y in range(0, height, 2):
            derive_z(depth - 1, y, ahead=halo(halo_z, y))

    def pass_y(t):
        for dz in range(2):
            for y in range(1 - dz, height, 2):
                derive_y(2 * t + dz, y)

    def pick(k):
        return v_ref if k == 0 else left.at[k - 1]

    def contract(outer, chunk, ref, lo, hi, base, fresh):
        sites = [
            (chunk * span + dz, y, c)
            for dz in range(span)
            for y in (range(height) if ref is trans_a else range(1 - dz % 2, height, 2))
            for c in range(3)
        ]
        a = jnp.concatenate(
            [ref[z, y if ref is trans_a else y // 2, c, lo:hi] for z, y, c in sites], axis=1
        )
        b = jnp.concatenate(
            [
                jnp.concatenate([pick(outer * 2 + s)[z, y, c] for z, y, c in sites], axis=1)
                for s in range(2)
            ],
            axis=0,
        )
        product = lax.dot_general(
            a, b, (((1,), (1,)), ((), ())), preferred_element_type=jnp.float32
        )
        columns = slice(outer * two, (outer + 1) * two)
        if fresh:
            acc[base + lo : base + hi, columns] = product
        else:
            acc[base + lo : base + hi, columns] += product

    half = 4 * rows

    def contract_far(step):
        fresh = step == 0
        first = chunk_at(step, pair) * span
        columns = slice(two, 2 * two)

        def add(ref, where, parts, sites):
            a = jnp.concatenate([jnp.concatenate(part, axis=1) for part in parts], axis=0)
            b = jnp.concatenate(
                [
                    jnp.concatenate([left[1 + s, z, y, c] for z, y, c in sites], axis=1)
                    for s in range(2)
                ],
                axis=0,
            )
            product = lax.dot_general(
                a, b, (((1,), (1,)), ((), ())), preferred_element_type=jnp.float32
            )
            if fresh:
                ref[where] = product
            else:
                ref[where] += product

        def sites_of(offset):
            return [
                (first + dz, y, c)
                for dz in range(span)
                for y in range((dz + offset) % 2, height, 2)
                for c in range(3)
            ]

        odd, even = sites_of(1), sites_of(0)
        add(
            acc,
            (slice(0, 2 * half), columns),
            [
                [trans_a[z, y, c] for z, y, c in odd],
                [trans_b[z, y // 2, c] for z, y, c in odd],
            ],
            odd,
        )
        if step < stretch:
            inner = (step * span) - first
            product_rows = [
                [trans_a[z, y, c] for z, y, c in even],
                [trans_c[z + inner, y // 2, c] for z, y, c in even],
            ]
            a = jnp.concatenate(
                [jnp.concatenate(part, axis=1) for part in product_rows], axis=0
            )
            b = jnp.concatenate(
                [
                    jnp.concatenate([left[1 + s, z, y, c] for z, y, c in even], axis=1)
                    for s in range(2)
                ],
                axis=0,
            )
            product = lax.dot_general(
                a, b, (((1,), (1,)), ((), ())), preferred_element_type=jnp.float32
            )
            acc[0:half, columns] += product[0:half]
            if fresh:
                acc_c[0:two] = product[0:two]
                acc_c[two:] = product[half:]
            else:
                acc_c[0:two] += product[0:two]
                acc_c[two:] += product[half:]

    def contract_all(outer, ref, lo, hi, base):
        contract(outer, 0, ref, lo, hi, base, True)
        pl.loop(1, chunks)(lambda k: contract(outer, k, ref, lo, hi, base, False))

    def turn_round(number):
        if number:
            heard(number - 1)
        greet(number)

    early = min(rounds, depth // 2)

    @pl.loop(0, depth)
    def _(z):
        for number in range(early):
            pl.when(z == 2 * number)(functools.partial(turn_round, number))
        pass_x(z)

    for number in range(early, rounds):
        turn_round(number)
    far[0].wait()
    relay[0].start()
    pl.loop(0, depth // 4)(pass_conjugate)
    pl.loop(0, depth // 2 - 1)(pass_z)
    heard(rounds - 1)
    rim_z_copy.start()
    for copy in z_copies:
        copy.start()
    near.wait()
    contract_all(0, trans_a, 0, half, 0)
    rim_y_copy.wait()

    @pl.loop(0, depth // 2)
    def _(t):
        put(edge_y, (2 * t + 1,), coefficients(rim_y[2 * t + 1]))

    for copy in y_copies:
        copy.wait()
    pl.loop(0, depth // 2)(pass_y)
    far[1].wait()
    relay[1].start()
    rim_z_copy.wait()
    for copy in z_copies:
        copy.wait()
    for y in range(1, height, 2):
        put(edge_z, (y,), coefficients(rim_z[y]))
    pass_z_edges()
    contract_all(0, trans_b, 0, half, half)

    left_half = lax.broadcasted_iota(jnp.int32, (1, two), 1) < rows
    kept_near, kept_far = side, pair

    def turn(value):
        return pltpu.roll(value, rows, 1)

    def exchange(stage, phase, step):
        source = outgo[stage].at[member(step)] if phase == 0 else reduced[stage]
        target = income[stage] if phase == 0 else gathered[stage]
        return pltpu.make_async_remote_copy(
            src_ref=source,
            dst_ref=target.at[me_g],
            send_sem=red_sem.at[stage, phase, 0, step],
            recv_sem=red_sem.at[stage, phase, 1, step],
            device_id=place(member(step)),
            device_id_type=MESH,
        )

    def cross(k, phase, step):
        if phase == 0:
            source, target = cross_out[k - 1].at[member(step)], cross_in[k - 1]
        else:
            source, target = back_out.at[k - 1], back_in.at[k - 1]
        return pltpu.make_async_remote_copy(
            src_ref=source,
            dst_ref=target.at[me_g],
            send_sem=cross_sem.at[k - 1, phase, 0, step],
            recv_sem=cross_sem.at[k - 1, phase, 1, step],
            device_id=place(member(step), k),
            device_id_type=MESH,
        )

    stage_partners = [(1,), (2, 3)]
    stage_rows = [
        [slot * rows for slot in range(8)],
        [slot * rows for slot in (0, 1, 2, 3, 4, 6)],
    ]

    def prepare(stage):
        columns = slice(stage * two, (stage + 1) * two)
        sent = []
        for op in range(2):
            base = half + op * two
            block = acc[base : base + two, columns]
            turned = jnp.transpose(block)
            if stage == 0:
                own = turned[0:rows]
                acc[base : base + rows, columns] = block[0:rows] - jnp.where(left_half, own, 0.0)
                acc[base + rows : base + two, columns] = block[rows:two] + jnp.where(
                    left_half, turn(own), 0.0
                )
                sent.append([turned[rows:two]])
            else:
                acc[base : base + rows, columns] = jnp.where(
                    kept_far == 0, block[0:rows], block[rows:two]
                )
                sent.append([turned[0:rows], turned[rows:two]])
        kept = kept_near if stage == 0 else kept_far
        for at, k in enumerate(stage_partners[stage]):
            first, second = sent[0][at], sent[1][at]
            if_real = jnp.where(left_half, -first, -turn(second))
            if_imag = jnp.where(left_half, turn(first), second)
            message = jnp.where(kept == 1, if_real, if_imag).astype(jnp.bfloat16)
            for g in range(group):
                cross_out[k - 1][g, 0:share] = message[g * share : (g + 1) * share]
        if stage == 1:
            for op in range(2):
                turned = jnp.transpose(acc_c[op * two : (op + 1) * two])
                flipped = -turned if op == 0 else turned
                message = jnp.where(left_half, flipped, -flipped).astype(jnp.bfloat16)
                for at, k in enumerate(stage_partners[stage]):
                    for g in range(group):
                        cross_out[k - 1][g, (op + 1) * share : (op + 2) * share] = message[
                            at * rows + g * share : at * rows + (g + 1) * share
                        ]

    def scatter_start(stage):
        columns = slice(stage * two, (stage + 1) * two)
        prepare(stage)
        for g in range(group):
            for at, row in enumerate(stage_rows[stage]):
                outgo[stage][g, at * share : (at + 1) * share] = acc[
                    row + g * share : row + (g + 1) * share, columns
                ].astype(jnp.bfloat16)
        for step in range(1, group):
            exchange(stage, 0, step).start()
        for k in stage_partners[stage]:
            for step in range(group):
                cross(k, 0, step).start()

    def gather_start(stage):
        columns = slice(stage * two, (stage + 1) * two)
        for step in range(1, group):
            exchange(stage, 0, step).wait()
        for k in stage_partners[stage]:
            for step in range(group):
                cross(k, 0, step).wait()
        parts = []
        for at, row in enumerate(stage_rows[stage]):
            if share % 8 == 0:
                mine = pl.ds(pl.multiple_of(row + me_g * share, share), share)
                total = acc[mine, columns]
            else:
                total = outgo[stage][me_g, at * share : (at + 1) * share].astype(jnp.float32)
            for step in range(1, group):
                total = total + income[stage][
                    member(step), at * share : (at + 1) * share
                ].astype(jnp.float32)
            parts.append(total)
        extra = []
        for k in stage_partners[stage]:
            total = cross_in[k - 1][0].astype(jnp.float32)
            for g in range(1, group):
                total = total + cross_in[k - 1][g].astype(jnp.float32)
            extra.append(total)
        if stage == 0:
            adds = [turn(extra[0]), extra[0]]
            for op in range(2):
                add = jnp.where(left_half, 0.0, adds[op])
                for part in range(2):
                    at = 4 + op * 2 + part
                    parts[at] = parts[at] + jnp.where(kept_near == part, add, 0.0)
            kept_of = [
                jnp.where(kept_near == 0, parts[4 + op * 2], parts[5 + op * 2]) for op in range(2)
            ]
            backs = [jnp.where(left_half, turn(kept_of[0]), kept_of[1])]
        else:
            for at in range(3):
                first, second = [total[at * share : (at + 1) * share] for total in extra]
                low, high = (4, 5) if at == 0 else (2 * at - 2, 2 * at - 1)
                parts[low] = parts[low] + jnp.where(left_half, first, turn(second))
                parts[high] = parts[high] + jnp.where(left_half, turn(first), second)
            backs = [
                jnp.where(left_half, parts[4], turn(parts[5])),
                jnp.where(left_half, turn(parts[4]), parts[5]),
            ]
        for at, total in enumerate(parts):
            rounded = total.astype(jnp.bfloat16)
            reduced[stage][at * share : (at + 1) * share] = rounded
            gathered[stage][me_g, at * share : (at + 1) * share] = rounded
        for k, back in zip(stage_partners[stage], backs):
            back_out[k - 1] = back.astype(jnp.bfloat16)
        for step in range(1, group):
            exchange(stage, 1, step).start()
        for k in stage_partners[stage]:
            for step in range(group):
                cross(k, 1, step).start()

    scale = 1.0 / math.sqrt(width * height * gy_n * depth * gz_n)

    def gather_finish(stage):
        for step in range(1, group):
            exchange(stage, 1, step).wait()
        for k in stage_partners[stage]:
            for step in range(group):
                cross(k, 1, step).wait()

        def slot(at):
            return jnp.concatenate(
                [
                    gathered[stage][g, at * share : (at + 1) * share].astype(jnp.float32)
                    for g in range(group)
                ],
                axis=0,
            )

        ks = stage_partners[stage]
        mirror = jnp.transpose(
            jnp.concatenate(
                [
                    back_in[k - 1, g].astype(jnp.float32)
                    for k in (ks if len(ks) == 2 else ks * 2)
                    for g in range(group)
                ],
                axis=0,
            )
        )
        full = [slot(at) for at in range(4)]
        for op in range(2):
            flipped = mirror[op * rows : (op + 1) * rows]
            for part in range(2):
                other = -flipped if part == 0 else flipped
                if stage == 0:
                    mine = slot(4 + op * 2 + part)
                    full.append(
                        jnp.where(left_half, mine, jnp.where(kept_near == part, mine, other))
                    )
                else:
                    full.append(jnp.where(kept_far == part, slot(4 + op), other))
        full = [jnp.where(side == 0, value, turn(value)) * scale for value in full]
        which = pair if stage == 0 else 1 - pair
        columns = pl.ds(pl.multiple_of(which * two, two), two)
        for part in range(2):
            along_x, phased, along_z, along_y = [full[2 * op + part] for op in range(4)]
            for op in range(3):
                chosen = directions_ref[op]
                out_ref[op * two + part * rows : op * two + (part + 1) * rows, columns] = jnp.where(
                    chosen == 0, along_x, jnp.where(chosen == 1, along_y, along_z)
                )
            out_ref[3 * two + part * rows : 3 * two + (part + 1) * rows, columns] = phased

    scatter_start(0)
    for k in range(2, chunks + 2):
        if k < chunks:
            far[k].wait()
            relay[k].start()
        relay[k - 2].wait()
        contract_far(k - 2)
    scatter_start(1)
    gather_start(0)
    gather_start(1)
    gather_finish(0)
    gather_finish(1)


def body(vectors, links, momentum, directions):
    rows, _, depth, height, lanes = vectors.shape
    gz_n = lax.axis_size("gz")
    gy_n = lax.axis_size("gy")
    vec_n = lax.axis_size("vec")
    group = gz_n * gy_n
    assert vec_n == 4 and depth % 4 == 0 and height % 2 == 0 and rows % group == 0
    chunks = split_chunks(depth, 4)
    v = jnp.transpose(vectors, (2, 3, 1, 0, 4))
    packed = jnp.transpose(links, (0, 3, 4, 1, 2, 5)).reshape(3, depth, height, 9, lanes)

    bf16, f32 = jnp.bfloat16, jnp.float32
    share = rows // group
    slots = (8, 6)
    far_count = chunks // 2 + depth // 2 * (height // 2)
    remote_count = 3 + depth + height + 2 * far_count
    vmem = pl.BlockSpec(memory_space=pltpu.VMEM)
    hbm = pl.BlockSpec(memory_space=pltpu.HBM)
    sizes = (gz_n, gy_n, vec_n, depth, height, rows, lanes // 2, chunks)
    parts = [pltpu.VMEM((group, n * share, 2 * rows), bf16) for n in slots]
    small = pltpu.VMEM((3, group, share, 2 * rows), bf16)
    crossing = [pltpu.VMEM((group, n * share, 2 * rows), bf16) for n in (1, 3, 3)]
    out = pl.pallas_call(
        functools.partial(kernel, sizes),
        out_shape=jax.ShapeDtypeStruct((8 * rows, vec_n * rows), f32),
        in_specs=[hbm, hbm, vmem, vmem],
        out_specs=vmem,
        scratch_shapes=[
            pltpu.VMEM((3, depth, height, 3, rows, lanes), bf16),
            pltpu.VMEM((depth, 3, rows, lanes), bf16),
            pltpu.VMEM((height, 3, rows, lanes), bf16),
            pltpu.VMEM((depth, 9, lanes), bf16),
            pltpu.VMEM((height, 9, lanes), bf16),
            pltpu.VMEM((2, depth, height, 32, lanes), f32),
            pltpu.VMEM((depth, height, 32, lanes), f32),
            pltpu.VMEM((depth, height, 32, lanes), f32),
            pltpu.VMEM((depth, 32, lanes), f32),
            pltpu.VMEM((height, 32, lanes), f32),
            pltpu.VMEM((depth * height, lanes), f32),
            pltpu.VMEM((depth * height, lanes), f32),
            pltpu.VMEM((depth, height, 3, 4 * rows, lanes), bf16),
            pltpu.VMEM((depth, height // 2, 3, 4 * rows, lanes), bf16),
            pltpu.VMEM((depth // 2, height // 2, 3, 2 * rows, lanes), bf16),
            pltpu.VMEM((8 * rows, vec_n * rows), f32),
            pltpu.VMEM((4 * rows, 2 * rows), f32),
            pltpu.SMEM((3,), jnp.int32),
            pltpu.SMEM((3,), jnp.int32),
            parts,
            parts,
            [pltpu.VMEM((n * share, 2 * rows), bf16) for n in slots],
            parts,
            crossing,
            crossing,
            pltpu.VMEM((3, share, 2 * rows), bf16),
            small,
            pltpu.SemaphoreType.DMA((2,)),
            pltpu.SemaphoreType.DMA((remote_count,)),
            pltpu.SemaphoreType.DMA((remote_count,)),
            pltpu.SemaphoreType.DMA((2, 2, 2, group)),
            pltpu.SemaphoreType.DMA((3, 2, 2, group)),
            pltpu.SemaphoreType.REGULAR((gy_n // 2 + gz_n,)),
        ],
        compiler_params=pltpu.CompilerParams(
            collective_id=0, has_side_effects=True, vmem_limit_bytes=48 * 1024 * 1024
        ),
    )(momentum, directions, v, packed)
    return out.reshape(4, 2, rows, vec_n * rows)


def solution(mesh):
    in_specs = (P("vec", None, "gz", "gy", None), P(None, None, None, "gz", "gy", None), P(), P())
    out_specs = P(None, None, "vec", None)
    return jax.shard_map(body, mesh=mesh, in_specs=in_specs, out_specs=out_specs, check_vma=False)
```
